32 devices in a mesh: pairs: 32 (over z, y, x, core).
Axes of the slice: x: 2, y: 2, z: 4, core: 2. Of those that a mesh axis runs over, the one named last changes fastest.
Arguments:
- pno_basis: bfloat16 [256, 192, 128], P('pairs'), may hold values from -0.4375 to 0.4375
- pno_count: int32 [256], P('pairs'), may hold values from 64 to 128
- partner_owner: int32 [256, 12], P('pairs'), may hold values from 0 to 31, all different within a row; in each aligned block of 8 rows (0 to 7, 8 to 15, ...) at most 3 rows name the same one
- partner_local: int32 [256, 12], P('pairs'), may hold values from 0 to 7
- exchange_k: bfloat16 [256, 128, 128], P('pairs'), may hold values from -6 to 6
- ladder_factor: bfloat16 [256, 40, 128, 128], P('pairs'), may hold values from -0.15625 to 0.15625
- pno_energy: float32 [256, 128], P('pairs'), may hold values from 0.3 to 3
- occ_energy: float32 [256], P('pairs'), may hold values from -2 to -0.6
- coupling_fock: bfloat16 [256, 12], P('pairs'), may hold values from -3 to 3
Outputs:
- amplitudes: float32 [256, 128, 128], P('pairs')
The draws below stay inside these ranges and needn't reach their ends.
Inputs may be any that keep to these rules, and one draw needn't show every extreme that they name: `partner_owner`: the 12 partners of one pair have different owners. Among the 8 pairs of one device no device is named more than 3 times, and in some devices' pairs one device is named exactly 3 times. Partner c of pair p is the pair numbered partner_owner[p, c] * 8 + partner_local[p, c]. Pair p uses its first pno_count[p] orbitals; the others are padding.
All inputs are finite; a program needn't handle non-finite values.
Results may differ from the reference program's by a relative error of at most 0.009.
Values may be sent and summed in bfloat16 or wider, within the bound.
A program may use at most 128 MiB of HBM per device.

```python
import math
import jax
import jax.numpy as jnp
import numpy as np
from jax import lax

NPNO = 128
NV = 192
NAUX = 40
NCOUP = 12
ITERS = 3
PAIRS_DEV = 8
PAIRS = 256
MOST = 3
N_PAIRS = 32


def set_ends(result, stream_key, smallest, top_value):
    extent = result.shape
    spot = [jax.random.randint(jax.random.fold_in(stream_key, axis), (), 0, extent[axis]) for axis in range(len(extent))]
    result = result.at[tuple(spot)].set(smallest)
    longest = extent.index(max(extent))
    spot[longest] = (spot[longest] + 1) % extent[longest]
    return result.at[tuple(spot)].set(top_value)


def block_levels(key, dims, shards, least, high):
    level = 1.0
    for dim, parts in shards:
        draws = jax.random.uniform(jax.random.fold_in(jax.random.fold_in(key, 6), dim), (parts,), jnp.float32, least / len(shards), high / len(shards))
        level = level * jnp.repeat(jnp.exp(draws), dims[dim] // parts).reshape((-1,) + (1,) * (len(dims) - 1 - dim))
    return level


def shared_out(rng, own, number, rows, amount, top, bound, skew):
    sequence = jax.random.permutation(rng, amount)
    packed, common = load_shares(amount, rows * top, bound, skew, True), load_shares(amount, rows * top, bound, skew, False)
    places = jnp.arange(amount)

    def named(sizes, turn):
        used = int((sizes > 0).sum())
        fixed = max(1, used // 4)
        passed = fixed + (places - fixed + turn * (used - fixed)) % max(1, amount - fixed)
        return jnp.zeros((amount,), jnp.int32).at[sequence[jnp.where(places < fixed, places, passed)]].set(jnp.asarray(sizes, jnp.int32))

    sizes = jnp.where(number % 4 == 0, named(packed, number // 4), named(common, number - number // 4 - 1))
    mixed = jax.random.permutation(jax.random.fold_in(own, 3), amount)
    giver, taker = mixed[0:amount // 2 * 2:2], mixed[1:amount // 2 * 2:2]
    room = jnp.minimum(sizes[giver] - 1, bound - sizes[taker]) // 2
    room = jnp.where((giver == sequence[0]) | (taker == sequence[0]) | (sizes[taker] == 0), 0, jnp.maximum(room, 0))
    passed = jax.random.randint(jax.random.fold_in(own, 4), (amount // 2,), 0, 1 << 20) % (room + 1)
    sizes = sizes.at[giver].add(-passed).at[taker].add(passed)
    labels = jnp.searchsorted(jnp.cumsum(sizes), jnp.arange(rows * top), side="right").astype(jnp.int32)
    table = labels.reshape(top, rows).T
    table = table[jax.random.permutation(jax.random.fold_in(own, 1), rows)]
    turn = jax.random.randint(jax.random.fold_in(own, 2), (rows, 1), 0, top)
    return jnp.take_along_axis(table, (jnp.arange(top)[None, :] + turn) % top, axis=1)


def load_shares(count, total, bound, lean, full):
    loads = [(1 << 20) // math.isqrt(grade ** lean) + 1 for grade in range(1, count + 1)]
    largest = bound if full else min(bound, max(-(-total // count), total * loads[0] // sum(loads)))
    least = 1 if total - largest >= count - 1 else 0
    given, rest = [largest] + [least] * (count - 1), total - largest - least * (count - 1)
    while rest > 0:
        candidates = [i for i in range(1, count) if given[i] < largest] or [i for i in range(1, count) if given[i] < bound]
        pool, remaining = sum([loads[i] for i in candidates]), rest
        for i in candidates:
            more = min(bound - given[i], max(1, remaining * loads[i] // pool), rest)
            given[i] = given[i] + more
            rest = rest - more
    return np.array(given)


def centred(own_key, extent, spread, limit, split=(), kind=jnp.bfloat16):
    result = jax.random.normal(own_key, extent, jnp.float32) * spread
    if len(split) > 0:
        result = block_levels(own_key, extent, split, -0.22, 0.18) * result
    return jnp.clip(result, min=-limit, max=limit).astype(kind)


def setup_inputs(seed: int = 0) -> dict:
    arg_keys = jax.random.split(jax.random.key(seed), 10)
    pno_basis = centred(arg_keys[0], (PAIRS, NV, NPNO), NV ** -0.5, 0.4375, ((0, 32),))
    pno_count = set_ends(jax.random.randint(arg_keys[1], (PAIRS,), NPNO // 2, NPNO + 1), jax.random.fold_in(arg_keys[1], 1), NPNO // 2, NPNO).astype(jnp.int32)
    partner_owner_keys = jax.random.split(jax.random.fold_in(arg_keys[2], 1), PAIRS // PAIRS_DEV)
    partner_owner_turns = jax.random.permutation(jax.random.fold_in(arg_keys[2], 3), PAIRS // PAIRS_DEV)
    partner_owner = jax.vmap(lambda own, number: shared_out(jax.random.fold_in(arg_keys[2], 2), own, number, PAIRS_DEV, N_PAIRS, NCOUP, MOST, 2))(partner_owner_keys, partner_owner_turns).reshape((PAIRS, NCOUP))
    partner_local = set_ends(jax.random.randint(arg_keys[3], (PAIRS, NCOUP), 0, PAIRS_DEV), jax.random.fold_in(arg_keys[3], 1), 0, PAIRS_DEV - 1).astype(jnp.int32)
    exchange_k = centred(arg_keys[4], (PAIRS, NPNO, NPNO), 1.0, 6.0, ((0, 32),))
    ladder_factor = centred(arg_keys[5], (PAIRS, NAUX, NPNO, NPNO), (NPNO * NAUX // 4) ** -0.5, 0.15625, ((0, 32),))
    pno_energy = jnp.clip(jnp.exp(math.log(3.0) - 2.3025851 * jax.random.uniform(arg_keys[6], (PAIRS, NPNO), jnp.float32) ** block_levels(arg_keys[6], (PAIRS, NPNO), ((0, 32),), -0.2, 0.2)), 0.3, 3.0)
    occ_energy = jnp.clip(-2.0 + 1.4 * jax.random.uniform(arg_keys[7], (PAIRS,), jnp.float32) ** block_levels(arg_keys[7], (PAIRS,), ((0, 32),), -0.2, 0.2), -2.0, -0.6)
    coupling_fock = centred(arg_keys[8], (PAIRS, NCOUP), 0.5, 3.0, ((0, 32),))
    return {"pno_basis": pno_basis, "pno_count": pno_count, "partner_owner": partner_owner, "partner_local": partner_local, "exchange_k": exchange_k, "ladder_factor": ladder_factor, "pno_energy": pno_energy, "occ_energy": occ_energy, "coupling_fock": coupling_fock}


level_shift = 0.3


def reference(pno_basis, pno_count, partner_owner, partner_local, exchange_k, ladder_factor, pno_energy, occ_energy, coupling_fock):
    columns = lax.broadcasted_iota(jnp.int32, (PAIRS, NPNO), 1)
    live_cols = (columns < pno_count[:, None]).astype(jnp.float32)
    masked_basis = (pno_basis.astype(jnp.float32) * live_cols[:, None, :]).astype(jnp.bfloat16)
    partner_ids = (partner_owner * PAIRS_DEV + partner_local).astype(jnp.int32)
    block_count = PAIRS // PAIRS_DEV
    block_numbers = jnp.arange(block_count, dtype=jnp.int32)

    def margin_block(block_index):
        first_row = (block_index * PAIRS_DEV).astype(jnp.int32)
        own_basis = lax.dynamic_slice_in_dim(masked_basis, first_row, PAIRS_DEV, 0).astype(jnp.float32)
        chosen = lax.dynamic_slice_in_dim(partner_ids, first_row, PAIRS_DEV, 0)
        other_basis = masked_basis[chosen].astype(jnp.float32)
        product = jnp.einsum("rva,rcvb->rcab", own_basis, other_basis, precision=lax.Precision.HIGHEST)
        return product.astype(jnp.bfloat16)

    margin = lax.map(margin_block, block_numbers).reshape(PAIRS, NCOUP, NPNO, NPNO)
    energy_sum = pno_energy[:, :, None] + pno_energy[:, None, :] - occ_energy[:, None, None]
    divisor = energy_sum + level_shift
    driving = exchange_k.astype(jnp.float32) * (live_cols[:, :, None] * live_cols[:, None, :])
    amplitudes = -driving / divisor
    weights = coupling_fock.astype(jnp.float32)
    for iteration in range(ITERS):
        sent_amps = amplitudes.astype(jnp.bfloat16)

        def couple_block(block_index):
            first_row = (block_index * PAIRS_DEV).astype(jnp.int32)
            block_margin = lax.dynamic_slice_in_dim(margin, first_row, PAIRS_DEV, 0).astype(jnp.float32)
            chosen = lax.dynamic_slice_in_dim(partner_ids, first_row, PAIRS_DEV, 0)
            block_weights = lax.dynamic_slice_in_dim(weights, first_row, PAIRS_DEV, 0)
            partner_amps = sent_amps[chosen].astype(jnp.float32)
            left_half = jnp.einsum("rcab,rcbd->rcad", block_margin, partner_amps, precision=lax.Precision.HIGHEST)
            left_half = left_half * block_weights[:, :, None, None]
            left_half = lax.optimization_barrier(left_half.astype(jnp.bfloat16)).astype(jnp.float32)
            coupling_terms = jnp.einsum("rcad,rced->rcae", left_half, block_margin, precision=lax.Precision.HIGHEST)
            coupling_terms = lax.optimization_barrier(coupling_terms.astype(jnp.bfloat16)).astype(jnp.float32)
            own_amps = lax.dynamic_slice_in_dim(sent_amps, first_row, PAIRS_DEV, 0).astype(jnp.float32)
            factors = lax.dynamic_slice_in_dim(ladder_factor, first_row, PAIRS_DEV, 0).astype(jnp.float32)
            ladder_half = jnp.einsum("rqac,rcd->rqad", factors, own_amps, precision=lax.Precision.HIGHEST)
            ladder_half = lax.optimization_barrier(ladder_half.astype(jnp.bfloat16)).astype(jnp.float32)
            ladder = jnp.einsum("rqad,rqbd->rab", ladder_half, factors, precision=lax.Precision.HIGHEST)
            return jnp.sum(coupling_terms, axis=1) + ladder

        coupled = lax.map(couple_block, block_numbers).reshape(PAIRS, NPNO, NPNO)
        residual = driving + energy_sum * amplitudes + coupled
        amplitudes = amplitudes - residual / divisor
    return amplitudes
```

```python
import jax
import jax.numpy as jnp
from jax import lax
from jax.sharding import PartitionSpec as P

ITERS = 3


level_shift = 0.3


def shards(
    pno_basis,
    pno_count,
    partner_owner,
    partner_local,
    exchange_k,
    ladder_factor,
    pno_energy,
    occ_energy,
    coupling_fock,
):
    own_pairs, domain, orbitals = pno_basis.shape
    fitted = ladder_factor.shape[1]
    partners = partner_owner.shape[1]
    listed = own_pairs * partners
    columns = lax.broadcasted_iota(jnp.int32, (own_pairs, orbitals), 1)
    live_cols = (columns < pno_count[:, None]).astype(jnp.float32)
    masked_basis = pno_basis * live_cols[:, None, :].astype(jnp.bfloat16)
    partner = (partner_owner * own_pairs + partner_local).reshape(listed)
    every_basis = lax.all_gather(masked_basis, "pairs", axis=0, tiled=True)
    partner_basis = every_basis[partner].reshape(own_pairs, partners, domain, orbitals)
    margin = jnp.einsum(
        "rva,rcvb->rcab", masked_basis, partner_basis, preferred_element_type=jnp.float32
    ).astype(jnp.bfloat16)
    energy_sum = pno_energy[:, :, None] + pno_energy[:, None, :] - occ_energy[:, None, None]
    divisor = energy_sum + level_shift
    driving = exchange_k.astype(jnp.float32) * (live_cols[:, :, None] * live_cols[:, None, :])
    amplitudes = -driving / divisor
    weights = coupling_fock.astype(jnp.float32)
    group_width = 8
    for iteration in range(ITERS):
        sent_amps = amplitudes.astype(jnp.bfloat16)
        every_amps = lax.all_gather(sent_amps, "pairs", axis=0, tiled=True)

        def add_group(group_index, total):
            factors = lax.dynamic_slice_in_dim(
                ladder_factor, group_index * group_width, group_width, 1
            )
            ladder_half = jnp.einsum(
                "rqac,rcd->rqad", factors, sent_amps, preferred_element_type=jnp.float32
            ).astype(jnp.bfloat16)
            return total + jnp.einsum(
                "rqad,rqbd->rab", ladder_half, factors, preferred_element_type=jnp.float32
            )

        ladder = lax.fori_loop(
            0,
            fitted // group_width,
            add_group,
            jnp.zeros((own_pairs, orbitals, orbitals), jnp.float32),
        )
        partner_amps = every_amps[partner]
        partner_amps = partner_amps.reshape(own_pairs, partners, orbitals, orbitals)
        left_half = jnp.einsum(
            "rcab,rcbd->rcad", margin, partner_amps, preferred_element_type=jnp.float32
        )
        left_half = (left_half * weights[:, :, None, None]).astype(jnp.bfloat16)
        gathered_terms = jnp.einsum(
            "rcad,rced->rcae", left_half, margin, preferred_element_type=jnp.float32
        ).astype(jnp.bfloat16)
        coupled = jnp.sum(gathered_terms, axis=1, dtype=jnp.float32)
        residual = driving + energy_sum * amplitudes + coupled + ladder
        amplitudes = amplitudes - residual / divisor
    return amplitudes


def solution(mesh):
    return jax.shard_map(
        shards,
        mesh=mesh,
        in_specs=(
            P("pairs", None, None),
            P("pairs"),
            P("pairs", None),
            P("pairs", None),
            P("pairs", None, None),
            P("pairs", None, None, None),
            P("pairs", None),
            P("pairs"),
            P("pairs", None),
        ),
        out_specs=P("pairs", None, None),
        check_vma=False,
    )
```

```python
import functools
import jax
import jax.numpy as jnp
from jax import lax
from jax.experimental import pallas as pl
from jax.experimental.pallas import tpu as pltpu
from jax.sharding import PartitionSpec as P

ITERS = 3


level_shift = 0.3
VMEM_BYTES = 67043328
MESH = pl.DeviceIdType.MESH


def contract(a, b, da, db):
    return lax.dot_general(a, b, (((da,), (db,)), ((), ())), preferred_element_type=jnp.float32)


def kernel(
    n, basis_ref, count_ref, owner_ref, local_ref, exchange_ref, ladder_hbm, energy_ref,
    energy_cols_ref, occ_ref, fock_ref, out_ref,
    all_basis, amps_a, amps_b, factors, margin, ladder,
    load_sem, recv_sem, recv_sib, send_z, send_near, send_sib,
):
    own_pairs, domain, orbitals = basis_ref.shape
    fitted = factors.shape[1]
    partners = owner_ref.shape[1]
    depth = n // 8
    stride = 8
    me = lax.axis_index("pairs")
    core = me % 2
    line = me // stride
    near = 2 + 2 * core
    far = 4 - 2 * core
    shift_near = near * (1 - 2 * ((me // 2 % 2) * (1 - core) + (me // 4 % 2) * core))
    shift_far = far * (1 - 2 * ((me // 4 % 2) * (1 - core) + (me // 2 % 2) * core))
    near_dev = me + shift_near
    far_dev = me + shift_far
    sibling = me + 1 - 2 * core
    bases = (me, near_dev, far_dev, me + shift_near + shift_far)
    tail = own_pairs // 4
    spans = ((0, own_pairs - tail), (own_pairs - tail, tail))
    rounds = (all_basis, amps_a, amps_b, amps_a)

    loads = [
        pltpu.make_async_copy(ladder_hbm.at[p], factors.at[p], load_sem.at[p])
        for p in range(own_pairs)
    ]
    for load in loads:
        load.start()

    def remote(r, t, owner, dev, ssem, rsem):
        lo, cnt = spans[t]
        view = rounds[r].at[owner, pl.ds(lo, cnt)]
        return pltpu.make_async_remote_copy(
            src_ref=view, dst_ref=view, send_sem=ssem, recv_sem=rsem,
            device_id=(dev,), device_id_type=MESH,
        )

    def send_line(r, t, owner, up):
        def go():
            remote(r, t, owner, me + stride * (1 if up else -1),
                   send_z.at[r % 2, int(up), t, owner // 2], recv_sem.at[r, t, owner // 2]).start()
        pl.when((line < depth - 1) if up else (line > 0))(go)

    def send_to(r, t, owner, which):
        dev = (near_dev, far_dev)[which]
        remote(r, t, owner, dev, send_near.at[r % 2, t, which], recv_sem.at[r, t, owner // 2]).start()

    def send_sibling(r, t, owner):
        remote(r, t, owner, sibling, send_sib.at[r % 2, t], recv_sib.at[r, t]).start()

    def forward(r, t, owner, via, up=None):
        if t == 0:
            if via in ("own", "line"):
                if up is None or up is False:
                    send_line(r, t, owner, False)
                if up is None or up is True:
                    send_line(r, t, owner, True)
                send_to(r, t, owner, 0)
            if via in ("own", "line", "near"):
                send_to(r, t, owner, 1)
        else:
            if via == "own":
                send_to(r, t, owner, 0)
            if via in ("own", "near"):
                send_to(r, t, owner, 1)
            if up is None or up is False:
                send_line(r, t, owner, False)
            if up is None or up is True:
                send_line(r, t, owner, True)
        send_sibling(r, t, owner)

    def arrive(r, t, owner, via, up=None):
        remote(r, t, owner, sibling, send_sib.at[r % 2, t], recv_sem.at[r, t, owner // 2]).wait_recv()
        forward(r, t, owner, via, up)

    def start_own(r):
        for t in (0, 1):
            forward(r, t, me, "own")

    vias = ("own", "near", "far", "far")

    def steps(r):
        found = []

        def at(t, b, k, up):
            def go():
                if k == 0:
                    arrive(r, t, bases[b], vias[b])
                else:
                    place = line + (k if up is False else -k)
                    owner = bases[b] + stride * (k if up is False else -k)

                    def inner():
                        if t == 0:
                            arrive(r, 0, owner, "line" if b == 0 else vias[b], up if b == 0 else None)
                        else:
                            arrive(r, 1, owner, "line", up)
                    pl.when((place >= 0) & (place < depth))(inner)
            found.append(go)

        for k in range(depth):
            for b in range(4):
                if k == 0:
                    if b == 0:
                        continue
                    at(1, b, 0, None)
                    at(0, b, 0, None)
                else:
                    for t in (0, 1):
                        for up in (True, False):
                            at(t, b, k, up)
        return found

    def run(r, pieces):
        todo = steps(r)
        done = 0
        for i, step in enumerate(todo):
            step()
            upto = len(pieces) * (i + 1) // len(todo)
            for piece in pieces[done:upto]:
                piece()
            done = upto
        whole(r, 0, n // 2, recv_sib.at[r, 0])
        whole(r, 1, n // 2, recv_sib.at[r, 1])

    def whole(r, t, number, sem):
        lo, cnt = spans[t]
        view = rounds[r].at[pl.ds(0, number), pl.ds(lo, cnt)]
        pltpu.make_async_copy(view, view, sem).wait()

    def finish_sends(r):
        for t in (0, 1):
            whole(r, t, depth if t == 0 else 1, send_near.at[r % 2, t, 0])
            whole(r, t, 2 * depth if t == 0 else 2, send_near.at[r % 2, t, 1])
            whole(r, t, n // 2, send_sib.at[r % 2, t])
            for b in range(1 if t == 0 else 4):
                for up in (True, False):
                    for j in range(depth):
                        owner = bases[b] + stride * (j - line)

                        def go(owner=owner, up=up, t=t):
                            remote(r, t, owner, sibling, send_z.at[r % 2, int(up), t, owner // 2],
                                   recv_sem.at[r, t, owner // 2]).wait_send()
                        pl.when(((line < depth - 1) & (j <= line)) if up else ((line > 0) & (j >= line)))(go)

    lanes = lax.broadcasted_iota(jnp.int32, (orbitals, orbitals), 1)
    rows = lax.broadcasted_iota(jnp.int32, (orbitals, orbitals), 0)

    def pair_terms(p):
        esum = energy_cols_ref[:, p : p + 1] + energy_ref[p : p + 1, :] - occ_ref[p]
        count = count_ref[p]
        live = (lanes < count) & (rows < count)
        driving = jnp.where(live, exchange_ref[p].astype(jnp.float32), 0.0)
        return esum, esum + level_shift, driving

    basis_lanes = lax.broadcasted_iota(jnp.int32, (domain, orbitals), 1)
    for p in range(own_pairs):
        all_basis[me, p] = jnp.where(
            basis_lanes < count_ref[p], basis_ref[p].astype(jnp.float32), 0.0
        ).astype(jnp.bfloat16)
        esum, divisor, driving = pair_terms(p)
        first = -driving / divisor
        out_ref[p] = first
        rounds[1][me, p] = first.astype(jnp.bfloat16)

    barrier = pltpu.get_barrier_semaphore()
    for dev in (near_dev, far_dev, sibling):
        pl.semaphore_signal(barrier, inc=1, device_id=(dev,), device_id_type=MESH)

    @pl.when(line > 0)
    def _():
        pl.semaphore_signal(barrier, inc=1, device_id=(me - stride,), device_id_type=MESH)

    @pl.when(line < depth - 1)
    def _():
        pl.semaphore_signal(barrier, inc=1, device_id=(me + stride,), device_id_type=MESH)

    @pl.when((line > 0) & (line < depth - 1))
    def _():
        pl.semaphore_wait(barrier, 5)

    @pl.when((line == 0) | (line == depth - 1))
    def _():
        pl.semaphore_wait(barrier, 4)

    group = 10 if fitted % 10 == 0 else 2

    def ladder_piece(r, p, first):
        def piece():
            if first:
                loads[p].wait()
            held = rounds[r][me, p]

            def body(g, total):
                for q in range(0, group, 2):
                    one = factors[p, g * group + q]
                    two = factors[p, g * group + q + 1]
                    half = jnp.concatenate(
                        [contract(one, held, 1, 0), contract(two, held, 1, 0)], axis=1
                    ).astype(jnp.bfloat16)
                    total = total + contract(half, jnp.concatenate([one, two], axis=1), 1, 1)
                return total

            ladder[p] = lax.fori_loop(
                0, fitted // group, body, jnp.zeros((orbitals, orbitals), jnp.float32)
            )
        return piece

    def margin_piece(p):
        def piece():
            flipped = jnp.transpose(all_basis[me, p].astype(jnp.float32)).astype(jnp.bfloat16)
            for c in range(partners):
                other = all_basis[owner_ref[p, c], local_ref[p, c]]
                margin[p, :, c * orbitals : (c + 1) * orbitals] = contract(
                    flipped, other, 1, 0
                ).astype(jnp.bfloat16)
        return piece

    def couple(r, p):
        amps = rounds[r]
        total = ladder[p]
        for c in range(0, partners, 2):
            both = margin[p, :, c * orbitals : (c + 2) * orbitals]
            lefts = []
            for d in (c, c + 1):
                block = amps[owner_ref[p, d], local_ref[p, d]]
                lefts.append(
                    contract(both[:, (d - c) * orbitals : (d - c + 1) * orbitals], block, 1, 0)
                    * fock_ref[p, d]
                )
            left = jnp.concatenate(lefts, axis=1).astype(jnp.bfloat16)
            total = total + contract(left, both, 1, 1)
        esum, divisor, driving = pair_terms(p)
        amplitudes = out_ref[p]
        residual = driving + esum * amplitudes + total
        amplitudes = amplitudes - residual / divisor
        out_ref[p] = amplitudes
        if r < ITERS:
            rounds[r + 1][me, p] = amplitudes.astype(jnp.bfloat16)

    start_own(0)
    start_own(1)
    run(0, [ladder_piece(1, p, True) for p in range(own_pairs)])
    for r in range(1, ITERS + 1):
        if r == 1:
            run(r, [margin_piece(p) for p in range(own_pairs)])
            finish_sends(0)
        else:
            run(r, [ladder_piece(r, p, False) for p in range(own_pairs)])
        finish_sends(r)
        for p in range(own_pairs):
            couple(r, p)
        if r < ITERS:
            start_own(r + 1)


def fused(
    n, pno_basis, pno_count, partner_owner, partner_local, exchange_k, ladder_factor,
    pno_energy, occ_energy, coupling_fock,
):
    own_pairs, domain, orbitals = pno_basis.shape
    fitted = ladder_factor.shape[1]
    partners = partner_owner.shape[1]
    smem = pl.BlockSpec(memory_space=pltpu.SMEM)
    vmem = pl.BlockSpec(memory_space=pltpu.VMEM)
    depth = n // 8
    amps = pltpu.VMEM((n, own_pairs, orbitals, orbitals), jnp.bfloat16)
    return pl.pallas_call(
        functools.partial(kernel, n),
        out_shape=jax.ShapeDtypeStruct((own_pairs, orbitals, orbitals), jnp.float32),
        in_specs=[vmem, smem, smem, smem, vmem, pl.BlockSpec(memory_space=pl.ANY), vmem, vmem, smem, smem],
        out_specs=vmem,
        scratch_shapes=[
            pltpu.VMEM((n, own_pairs, domain, orbitals), jnp.bfloat16),
            amps,
            amps,
            pltpu.VMEM(ladder_factor.shape, jnp.bfloat16),
            pltpu.VMEM((own_pairs, orbitals, partners * orbitals), jnp.bfloat16),
            pltpu.VMEM((own_pairs, orbitals, orbitals), jnp.float32),
            pltpu.SemaphoreType.DMA((own_pairs,)),
            pltpu.SemaphoreType.DMA((ITERS + 1, 2, n // 2)),
            pltpu.SemaphoreType.DMA((ITERS + 1, 2)),
            pltpu.SemaphoreType.DMA((2, 2, 2, n // 2)),
            pltpu.SemaphoreType.DMA((2, 2, 2)),
            pltpu.SemaphoreType.DMA((2, 2)),
        ],
        compiler_params=pltpu.CompilerParams(
            collective_id=0, has_side_effects=True, vmem_limit_bytes=VMEM_BYTES
        ),
        name="jacobi",
    )(
        pno_basis, pno_count, partner_owner, partner_local, exchange_k, ladder_factor,
        pno_energy, pno_energy.T, occ_energy, coupling_fock.astype(jnp.float32),
    )


def shards(*args):
    n = lax.axis_size("pairs")
    own_pairs, domain, orbitals = args[0].shape
    gathered = n * own_pairs * orbitals * (domain + 2 * orbitals) * 2
    resident = args[5].size * 2 + own_pairs * orbitals * orbitals * (2 * args[2].shape[1] + 16)
    fits = gathered + resident < VMEM_BYTES - (4 << 20)
    if n % 16 == 0 and own_pairs % 4 == 0 and args[2].shape[1] % 2 == 0 and fits:
        return fused(n, *args)
    return gathered_rows(*args)


def gathered_rows(
    pno_basis,
    pno_count,
    partner_owner,
    partner_local,
    exchange_k,
    ladder_factor,
    pno_energy,
    occ_energy,
    coupling_fock,
):
    own_pairs, domain, orbitals = pno_basis.shape
    fitted = ladder_factor.shape[1]
    partners = partner_owner.shape[1]
    listed = own_pairs * partners
    columns = lax.broadcasted_iota(jnp.int32, (own_pairs, orbitals), 1)
    live_cols = (columns < pno_count[:, None]).astype(jnp.float32)
    masked_basis = pno_basis * live_cols[:, None, :].astype(jnp.bfloat16)
    partner = (partner_owner * own_pairs + partner_local).reshape(listed)
    every_basis = lax.all_gather(masked_basis, "pairs", axis=0, tiled=True)
    partner_basis = every_basis[partner].reshape(own_pairs, partners, domain, orbitals)
    margin = jnp.einsum(
        "rva,rcvb->rcab", masked_basis, partner_basis, preferred_element_type=jnp.float32
    ).astype(jnp.bfloat16)
    energy_sum = pno_energy[:, :, None] + pno_energy[:, None, :] - occ_energy[:, None, None]
    divisor = energy_sum + level_shift
    driving = exchange_k.astype(jnp.float32) * (live_cols[:, :, None] * live_cols[:, None, :])
    amplitudes = -driving / divisor
    weights = coupling_fock.astype(jnp.float32)
    group_width = 8
    for iteration in range(ITERS):
        sent_amps = amplitudes.astype(jnp.bfloat16)
        every_amps = lax.all_gather(sent_amps, "pairs", axis=0, tiled=True)

        def add_group(group_index, total):
            factors = lax.dynamic_slice_in_dim(
                ladder_factor, group_index * group_width, group_width, 1
            )
            ladder_half = jnp.einsum(
                "rqac,rcd->rqad", factors, sent_amps, preferred_element_type=jnp.float32
            ).astype(jnp.bfloat16)
            return total + jnp.einsum(
                "rqad,rqbd->rab", ladder_half, factors, preferred_element_type=jnp.float32
            )

        ladder = lax.fori_loop(
            0,
            fitted // group_width,
            add_group,
            jnp.zeros((own_pairs, orbitals, orbitals), jnp.float32),
        )
        partner_amps = every_amps[partner]
        partner_amps = partner_amps.reshape(own_pairs, partners, orbitals, orbitals)
        left_half = jnp.einsum(
            "rcab,rcbd->rcad", margin, partner_amps, preferred_element_type=jnp.float32
        )
        left_half = (left_half * weights[:, :, None, None]).astype(jnp.bfloat16)
        gathered_terms = jnp.einsum(
            "rcad,rced->rcae", left_half, margin, preferred_element_type=jnp.float32
        ).astype(jnp.bfloat16)
        coupled = jnp.sum(gathered_terms, axis=1, dtype=jnp.float32)
        residual = driving + energy_sum * amplitudes + coupled + ladder
        amplitudes = amplitudes - residual / divisor
    return amplitudes


def solution(mesh):
    return jax.shard_map(
        shards,
        mesh=mesh,
        in_specs=(
            P("pairs", None, None),
            P("pairs"),
            P("pairs", None),
            P("pairs", None),
            P("pairs", None, None),
            P("pairs", None, None, None),
            P("pairs", None),
            P("pairs"),
            P("pairs", None),
        ),
        out_specs=P("pairs", None, None),
        check_vma=False,
    )
```

```python
import functools
import jax
import jax.numpy as jnp
from jax import lax
from jax.experimental import pallas as pl
from jax.experimental.pallas import tpu as pltpu
from jax.sharding import PartitionSpec as P

ITERS = 3


level_shift = 0.3
VMEM_BYTES = 67043328
MESH = pl.DeviceIdType.MESH


def contract(a, b, da, db):
    return lax.dot_general(a, b, (((da,), (db,)), ((), ())), preferred_element_type=jnp.float32)


def kernel(
    n, basis_ref, count_ref, owner_ref, local_ref, exchange_ref, ladder_hbm, energy_ref,
    energy_cols_ref, occ_ref, fock_ref, out_ref,
    all_basis, amps_a, amps_b, factors, margin, ladder,
    load_sem, recv_sem, recv_sib, send_z, send_near, send_sib,
):
    own_pairs, domain, orbitals = basis_ref.shape
    fitted = factors.shape[1]
    partners = owner_ref.shape[1]
    depth = n // 8
    stride = 8
    me = lax.axis_index("pairs")
    core = me % 2
    line = me // stride
    near = 2 + 2 * core
    far = 4 - 2 * core
    shift_near = near * (1 - 2 * ((me // 2 % 2) * (1 - core) + (me // 4 % 2) * core))
    shift_far = far * (1 - 2 * ((me // 4 % 2) * (1 - core) + (me // 2 % 2) * core))
    near_dev = me + shift_near
    far_dev = me + shift_far
    sibling = me + 1 - 2 * core
    bases = (me, near_dev, far_dev, me + shift_near + shift_far)
    tail = own_pairs // 4
    half = (own_pairs - tail) // 2
    spans = ((0, half), (half, own_pairs - tail - half), (own_pairs - tail, tail))
    kinds = (0, 0, 1)
    rounds = (all_basis, amps_a, amps_b, amps_a)

    loads = [
        pltpu.make_async_copy(ladder_hbm.at[p], factors.at[p], load_sem.at[p])
        for p in range(own_pairs)
    ]
    for load in loads:
        load.start()

    def remote(r, t, owner, dev, ssem, rsem):
        lo, cnt = spans[t]
        view = rounds[r].at[owner, pl.ds(lo, cnt)]
        return pltpu.make_async_remote_copy(
            src_ref=view, dst_ref=view, send_sem=ssem, recv_sem=rsem,
            device_id=(dev,), device_id_type=MESH,
        )

    def send_line(r, t, owner, up):
        def go():
            remote(r, t, owner, me + stride * (1 if up else -1),
                   send_z.at[r % 2, int(up), t, owner // 2], recv_sem.at[r, t, owner // 2]).start()
        pl.when((line < depth - 1) if up else (line > 0))(go)

    def send_to(r, t, owner, which):
        dev = (near_dev, far_dev)[which]
        remote(r, t, owner, dev, send_near.at[r % 2, t, which], recv_sem.at[r, t, owner // 2]).start()

    def send_sibling(r, t, owner):
        remote(r, t, owner, sibling, send_sib.at[r % 2, t], recv_sib.at[r, t]).start()

    def forward(r, t, owner, via, up=None):
        if kinds[t] == 0:
            if via in ("own", "line"):
                if up is None or up is False:
                    send_line(r, t, owner, False)
                if up is None or up is True:
                    send_line(r, t, owner, True)
                send_to(r, t, owner, 0)
            if via in ("own", "line", "near"):
                send_to(r, t, owner, 1)
        else:
            if via == "own":
                send_to(r, t, owner, 0)
            if via in ("own", "near"):
                send_to(r, t, owner, 1)
            if up is None or up is False:
                send_line(r, t, owner, False)
            if up is None or up is True:
                send_line(r, t, owner, True)
        send_sibling(r, t, owner)

    def arrive(r, t, owner, via, up=None):
        remote(r, t, owner, sibling, send_sib.at[r % 2, t], recv_sem.at[r, t, owner // 2]).wait_recv()
        forward(r, t, owner, via, up)

    def start_own(r):
        for t in reversed(range(len(spans))):
            forward(r, t, me, "own")

    vias = ("own", "near", "far", "far")

    def steps(r):
        found = []

        def at(t, b, k, up):
            def go():
                if k == 0:
                    arrive(r, t, bases[b], vias[b])
                else:
                    place = line + (k if up is False else -k)
                    owner = bases[b] + stride * (k if up is False else -k)

                    def inner():
                        if kinds[t] == 0:
                            arrive(r, t, owner, "line" if b == 0 else vias[b], up if b == 0 else None)
                        else:
                            arrive(r, t, owner, "line", up)
                    pl.when((place >= 0) & (place < depth))(inner)
            found.append(go)

        order = [(1, 1, 0), (0, 0, 1), (1, 2, 0), (0, 1, 0), (1, 3, 0), (1, 0, 1), (0, 0, 2), (0, 1, 1), (1, 1, 1), (1, 2, 1), (0, 0, 3), (1, 3, 1), (0, 1, 2)]
        order += [(1, 0, 2), (0, 2, 0), (1, 1, 2), (0, 3, 0), (0, 1, 3), (1, 2, 2), (0, 2, 1), (1, 3, 2), (0, 3, 1), (0, 2, 2), (1, 0, 3), (0, 3, 2), (1, 1, 3)]
        order = [event for event in order if event[2] < depth]
        every = [(t, b, k) for k in range(depth) for t in (0, 1) for b in (2, 3, 0, 1)]
        order += [event for event in every if event not in order and event != (0, 0, 0) and event != (1, 0, 0)]
        for kind, b, k in order:
            for t in range(len(spans)):
                for up in (None,) if k == 0 else (True, False):
                    if kinds[t] == kind:
                        at(t, b, k, up)
        return found

    def run(r, pieces):
        todo = steps(r)
        done = 0
        for i, step in enumerate(todo):
            step()
            upto = len(pieces) * (i + 1) // len(todo)
            for piece in pieces[done:upto]:
                piece()
            done = upto
        for t in range(len(spans)):
            whole(r, t, n // 2, recv_sib.at[r, t])

    def whole(r, t, number, sem):
        lo, cnt = spans[t]
        view = rounds[r].at[pl.ds(0, number), pl.ds(lo, cnt)]
        pltpu.make_async_copy(view, view, sem).wait()

    def finish_sends(r):
        for t in range(len(spans)):
            whole(r, t, depth if kinds[t] == 0 else 1, send_near.at[r % 2, t, 0])
            whole(r, t, 2 * depth if kinds[t] == 0 else 2, send_near.at[r % 2, t, 1])
            whole(r, t, n // 2, send_sib.at[r % 2, t])
            for b in range(1 if kinds[t] == 0 else 4):
                for up in (True, False):
                    for j in range(depth):
                        owner = bases[b] + stride * (j - line)

                        def go(owner=owner, up=up, t=t):
                            remote(r, t, owner, sibling, send_z.at[r % 2, int(up), t, owner // 2],
                                   recv_sem.at[r, t, owner // 2]).wait_send()
                        pl.when(((line < depth - 1) & (j <= line)) if up else ((line > 0) & (j >= line)))(go)

    lanes = lax.broadcasted_iota(jnp.int32, (orbitals, orbitals), 1)
    rows = lax.broadcasted_iota(jnp.int32, (orbitals, orbitals), 0)

    def pair_terms(p):
        esum = energy_cols_ref[:, p : p + 1] + energy_ref[p : p + 1, :] - occ_ref[p]
        count = count_ref[p]
        live = (lanes < count) & (rows < count)
        driving = jnp.where(live, exchange_ref[p].astype(jnp.float32), 0.0)
        return esum, esum + level_shift, driving

    basis_lanes = lax.broadcasted_iota(jnp.int32, (domain, orbitals), 1)
    for p in range(own_pairs):
        all_basis[me, p] = jnp.where(
            basis_lanes < count_ref[p], basis_ref[p].astype(jnp.float32), 0.0
        ).astype(jnp.bfloat16)
        esum, divisor, driving = pair_terms(p)
        first = -driving / divisor
        out_ref[p] = first
        rounds[1][me, p] = first.astype(jnp.bfloat16)

    barrier = pltpu.get_barrier_semaphore()
    for dev in (near_dev, far_dev, sibling):
        pl.semaphore_signal(barrier, inc=1, device_id=(dev,), device_id_type=MESH)

    @pl.when(line > 0)
    def _():
        pl.semaphore_signal(barrier, inc=1, device_id=(me - stride,), device_id_type=MESH)

    @pl.when(line < depth - 1)
    def _():
        pl.semaphore_signal(barrier, inc=1, device_id=(me + stride,), device_id_type=MESH)

    @pl.when((line > 0) & (line < depth - 1))
    def _():
        pl.semaphore_wait(barrier, 5)

    @pl.when((line == 0) | (line == depth - 1))
    def _():
        pl.semaphore_wait(barrier, 4)

    group = 10 if fitted % 10 == 0 else 2

    def ladder_piece(r, p, first):
        def piece():
            if first:
                loads[p].wait()
            held = rounds[r][me, p]

            def body(g, total):
                for q in range(0, group, 2):
                    one = factors[p, g * group + q]
                    two = factors[p, g * group + q + 1]
                    half = jnp.concatenate(
                        [contract(one, held, 1, 0), contract(two, held, 1, 0)], axis=1
                    ).astype(jnp.bfloat16)
                    total = total + contract(half, jnp.concatenate([one, two], axis=1), 1, 1)
                return total

            ladder[p] = lax.fori_loop(
                0, fitted // group, body, jnp.zeros((orbitals, orbitals), jnp.float32)
            )
        return piece

    def margin_piece(p):
        def piece():
            flipped = jnp.transpose(all_basis[me, p].astype(jnp.float32)).astype(jnp.bfloat16)
            for c in range(partners):
                other = all_basis[owner_ref[p, c], local_ref[p, c]]
                margin[p, :, c * orbitals : (c + 1) * orbitals] = contract(
                    flipped, other, 1, 0
                ).astype(jnp.bfloat16)
        return piece

    def couple(r, p):
        amps = rounds[r]
        total = ladder[p]
        for c in range(0, partners, 2):
            both = margin[p, :, c * orbitals : (c + 2) * orbitals]
            lefts = []
            for d in (c, c + 1):
                block = amps[owner_ref[p, d], local_ref[p, d]]
                lefts.append(
                    contract(both[:, (d - c) * orbitals : (d - c + 1) * orbitals], block, 1, 0)
                    * fock_ref[p, d]
                )
            left = jnp.concatenate(lefts, axis=1).astype(jnp.bfloat16)
            total = total + contract(left, both, 1, 1)
        esum, divisor, driving = pair_terms(p)
        amplitudes = out_ref[p]
        residual = driving + esum * amplitudes + total
        amplitudes = amplitudes - residual / divisor
        out_ref[p] = amplitudes
        if r < ITERS:
            rounds[r + 1][me, p] = amplitudes.astype(jnp.bfloat16)

    start_own(0)
    start_own(1)
    run(0, [ladder_piece(1, p, True) for p in range(own_pairs)])
    for r in range(1, ITERS + 1):
        if r == 1:
            run(r, [margin_piece(p) for p in range(own_pairs)])
        else:
            run(r, [ladder_piece(r, p, False) for p in range(own_pairs)])
        if r == 1:
            finish_sends(0)
        for t in reversed(range(len(spans))):
            for p in range(spans[t][0], spans[t][0] + spans[t][1]):
                couple(r, p)
            if t == 0:
                finish_sends(r)
            if r < ITERS:
                forward(r + 1, t, me, "own")


def fused(
    n, pno_basis, pno_count, partner_owner, partner_local, exchange_k, ladder_factor,
    pno_energy, occ_energy, coupling_fock,
):
    own_pairs, domain, orbitals = pno_basis.shape
    fitted = ladder_factor.shape[1]
    partners = partner_owner.shape[1]
    smem = pl.BlockSpec(memory_space=pltpu.SMEM)
    vmem = pl.BlockSpec(memory_space=pltpu.VMEM)
    depth = n // 8
    amps = pltpu.VMEM((n, own_pairs, orbitals, orbitals), jnp.bfloat16)
    return pl.pallas_call(
        functools.partial(kernel, n),
        out_shape=jax.ShapeDtypeStruct((own_pairs, orbitals, orbitals), jnp.float32),
        in_specs=[vmem, smem, smem, smem, vmem, pl.BlockSpec(memory_space=pl.ANY), vmem, vmem, smem, smem],
        out_specs=vmem,
        scratch_shapes=[
            pltpu.VMEM((n, own_pairs, domain, orbitals), jnp.bfloat16),
            amps,
            amps,
            pltpu.VMEM(ladder_factor.shape, jnp.bfloat16),
            pltpu.VMEM((own_pairs, orbitals, partners * orbitals), jnp.bfloat16),
            pltpu.VMEM((own_pairs, orbitals, orbitals), jnp.float32),
            pltpu.SemaphoreType.DMA((own_pairs,)),
            pltpu.SemaphoreType.DMA((ITERS + 1, 3, n // 2)),
            pltpu.SemaphoreType.DMA((ITERS + 1, 3)),
            pltpu.SemaphoreType.DMA((2, 2, 3, n // 2)),
            pltpu.SemaphoreType.DMA((2, 3, 2)),
            pltpu.SemaphoreType.DMA((2, 3)),
        ],
        compiler_params=pltpu.CompilerParams(
            collective_id=0, has_side_effects=True, vmem_limit_bytes=VMEM_BYTES
        ),
        name="jacobi",
    )(
        pno_basis, pno_count, partner_owner, partner_local, exchange_k, ladder_factor,
        pno_energy, pno_energy.T, occ_energy, coupling_fock.astype(jnp.float32),
    )


def shards(*args):
    n = lax.axis_size("pairs")
    own_pairs, domain, orbitals = args[0].shape
    gathered = n * own_pairs * orbitals * (domain + 2 * orbitals) * 2
    resident = args[5].size * 2 + own_pairs * orbitals * orbitals * (2 * args[2].shape[1] + 16)
    fits = gathered + resident < VMEM_BYTES - (4 << 20)
    if n % 16 == 0 and own_pairs % 4 == 0 and args[2].shape[1] % 2 == 0 and fits:
        return fused(n, *args)
    return gathered_rows(*args)


def gathered_rows(
    pno_basis,
    pno_count,
    partner_owner,
    partner_local,
    exchange_k,
    ladder_factor,
    pno_energy,
    occ_energy,
    coupling_fock,
):
    own_pairs, domain, orbitals = pno_basis.shape
    fitted = ladder_factor.shape[1]
    partners = partner_owner.shape[1]
    listed = own_pairs * partners
    columns = lax.broadcasted_iota(jnp.int32, (own_pairs, orbitals), 1)
    live_cols = (columns < pno_count[:, None]).astype(jnp.float32)
    masked_basis = pno_basis * live_cols[:, None, :].astype(jnp.bfloat16)
    partner = (partner_owner * own_pairs + partner_local).reshape(listed)
    every_basis = lax.all_gather(masked_basis, "pairs", axis=0, tiled=True)
    partner_basis = every_basis[partner].reshape(own_pairs, partners, domain, orbitals)
    margin = jnp.einsum(
        "rva,rcvb->rcab", masked_basis, partner_basis, preferred_element_type=jnp.float32
    ).astype(jnp.bfloat16)
    energy_sum = pno_energy[:, :, None] + pno_energy[:, None, :] - occ_energy[:, None, None]
    divisor = energy_sum + level_shift
    driving = exchange_k.astype(jnp.float32) * (live_cols[:, :, None] * live_cols[:, None, :])
    amplitudes = -driving / divisor
    weights = coupling_fock.astype(jnp.float32)
    group_width = 8
    for iteration in range(ITERS):
        sent_amps = amplitudes.astype(jnp.bfloat16)
        every_amps = lax.all_gather(sent_amps, "pairs", axis=0, tiled=True)

        def add_group(group_index, total):
            factors = lax.dynamic_slice_in_dim(
                ladder_factor, group_index * group_width, group_width, 1
            )
            ladder_half = jnp.einsum(
                "rqac,rcd->rqad", factors, sent_amps, preferred_element_type=jnp.float32
            ).astype(jnp.bfloat16)
            return total + jnp.einsum(
                "rqad,rqbd->rab", ladder_half, factors, preferred_element_type=jnp.float32
            )

        ladder = lax.fori_loop(
            0,
            fitted // group_width,
            add_group,
            jnp.zeros((own_pairs, orbitals, orbitals), jnp.float32),
        )
        partner_amps = every_amps[partner]
        partner_amps = partner_amps.reshape(own_pairs, partners, orbitals, orbitals)
        left_half = jnp.einsum(
            "rcab,rcbd->rcad", margin, partner_amps, preferred_element_type=jnp.float32
        )
        left_half = (left_half * weights[:, :, None, None]).astype(jnp.bfloat16)
        gathered_terms = jnp.einsum(
            "rcad,rced->rcae", left_half, margin, preferred_element_type=jnp.float32
        ).astype(jnp.bfloat16)
        coupled = jnp.sum(gathered_terms, axis=1, dtype=jnp.float32)
        residual = driving + energy_sum * amplitudes + coupled + ladder
        amplitudes = amplitudes - residual / divisor
    return amplitudes


def solution(mesh):
    return jax.shard_map(
        shards,
        mesh=mesh,
        in_specs=(
            P("pairs", None, None),
            P("pairs"),
            P("pairs", None),
            P("pairs", None),
            P("pairs", None, None),
            P("pairs", None, None, None),
            P("pairs", None),
            P("pairs"),
            P("pairs", None),
        ),
        out_specs=P("pairs", None, None),
        check_vma=False,
    )
```
